512 devices in a mesh: sector: 16 (over z), dir: 32 (over y, x, core).
Axes of the slice: x: 4, y: 4, z: 16, core: 2. Of those that a mesh axis runs over, the one named last changes fastest.
Arguments:
- fields: bfloat16 [16384, 128, 128], P(('sector', 'dir')), may hold values from -6 to 6
- aggregation: bfloat16 [64, 256], replicated, may hold values from -0.375 to 0.375
- operators: bfloat16 [64, 64, 64, 128], P(None, 'dir'), may hold values from -0.09375 to 0.09375
- disaggregation: bfloat16 [128, 128], replicated, may hold values from -0.5 to 0.5
- near_tile: int32 [256, 16], P('sector'), may hold values from 0 to 15
- near_operator: int32 [256, 16], P('sector'), may hold values from 0 to 63
- far_slot: int32 [256, 16], P('sector'), may hold values from 0 to 31, as said below
- far_operator: int32 [256, 16], P('sector'), may hold values from 0 to 63
- send_tiles: int32 [16, 16, 2], replicated, may hold values from 0 to 15, as said below
Outputs:
- scattered: bfloat16 [16384, 128, 128], P(('sector', 'dir'))
The draws below stay inside these ranges and needn't reach their ends.
Inputs may be any that keep to these rules, and one draw needn't show every extreme that they name: `send_tiles`: for every source and target sector the 2 entries are distinct tile numbers within the source sector. `far_slot`: entry c * 2 + j names slot j of the list that sector c keeps for the target tile's sector; c is never the target tile's own sector.
All inputs are finite; a program needn't handle non-finite values.
Results may differ from the reference program's by a relative error of at most 0.0058.
Values may be sent and summed in bfloat16 or wider, within the bound.
A program may use at most 128 MiB of HBM per device.

```python
import jax
import jax.numpy as jnp
from jax import lax

Q = 128
K = 64
ILL = 64
TILE = 64
NOPS = 64
LNEAR = 16
LFAR = 16
CAP = 2
BOXES = 16384
TPS = 16
NTILES = 256


def draw_send_tiles(key, part):
    sectors = NTILES // TPS
    subkeys = jax.random.split(jax.random.fold_in(key, 11), sectors * sectors)
    orders = jax.vmap(lambda sub: jax.random.permutation(sub, TPS)[:CAP])(subkeys)
    return orders.reshape(sectors, sectors, CAP).astype(jnp.int32)


def draw_far_slot(key, part):
    sectors = NTILES // TPS
    base = jax.random.fold_in(key, 23)
    key_one, key_two, key_three = jax.random.split(base, 3)
    own_sector = (jnp.arange(NTILES, dtype=jnp.int32) // TPS)[:, None]
    first_pick = jax.random.randint(key_one, (NTILES, LFAR), 0, sectors - 1)
    second_pick = jax.random.randint(key_two, (NTILES, LFAR), 0, sectors - 1)
    distance = jnp.minimum(first_pick, second_pick) + 1
    source = (own_sector + distance) % sectors
    position = jax.random.randint(key_three, (NTILES, LFAR), 0, CAP)
    return (source * CAP + position).astype(jnp.int32)


def set_ends(values, rng, low, largest):
    longest = values.shape.index(max(values.shape))
    spots = []
    for shift in (0, 1):
        where = [jax.random.randint(jax.random.fold_in(rng, axis), (), 0, length) for axis, length in enumerate(values.shape)]
        where[longest] = (where[longest] + shift) % values.shape[longest]
        spots.append(tuple(where))
    return values.at[spots[0]].set(low).at[spots[1]].set(largest)


def steps_of(key, extent, pieces, low, largest):
    loudness, own = 1.0, jax.random.fold_in(key, 6)
    for dim, parts in pieces:
        heights = jnp.exp(jax.random.uniform(jax.random.fold_in(own, dim), (parts,), jnp.float32, low / len(pieces), largest / len(pieces)))
        loudness = loudness * jnp.repeat(heights, extent[dim] // parts).reshape([-1 if axis == dim else 1 for axis in range(len(extent))])
    return loudness


def scatter_about(key, shape, deviation, limit, cuts=(), kind=jnp.bfloat16):
    drawn = jax.random.normal(key, shape, jnp.float32) * deviation
    if len(cuts) > 0:
        drawn = steps_of(key, shape, cuts, -0.22, 0.18) * drawn
    return jnp.clip(drawn, min=-limit, max=limit).astype(kind)


def setup_inputs(seed: int = 0) -> dict:
    key_list = jax.random.split(jax.random.key(seed), 10)
    return {
        "fields": scatter_about(key_list[0], (BOXES, Q, 2 * ILL), 1.0, 6.0, ((0, 512),)),
        "aggregation": scatter_about(key_list[1], (K, 2 * Q), (2 * Q) ** -0.5, 0.375),
        "operators": scatter_about(key_list[2], (NOPS, K, TILE, 2 * TILE), (2 * TILE * (LNEAR + LFAR)) ** -0.5, 0.09375, ((1, 32),)),
        "disaggregation": scatter_about(key_list[3], (Q, 2 * K), (2 * K) ** -0.5, 0.5),
        "near_tile": set_ends(jax.random.randint(key_list[4], (NTILES, LNEAR), 0, TPS), jax.random.fold_in(key_list[4], 1), 0, TPS - 1).astype(jnp.int32),
        "near_operator": set_ends(jax.random.randint(key_list[5], (NTILES, LNEAR), 0, NOPS), jax.random.fold_in(key_list[5], 1), 0, NOPS - 1).astype(jnp.int32),
        "far_slot": draw_far_slot(jax.random.fold_in(key_list[9], 71), 0),
        "far_operator": set_ends(jax.random.randint(key_list[7], (NTILES, LFAR), 0, NOPS), jax.random.fold_in(key_list[7], 1), 0, NOPS - 1).astype(jnp.int32),
        "send_tiles": draw_send_tiles(jax.random.fold_in(key_list[9], 71), 0),
    }


def stacked(values, axis):
    halfway = values.shape[-1] // 2
    lower_rows = jnp.concatenate([-values[..., halfway:], values[..., :halfway]], axis=-1)
    return jnp.concatenate([values, lower_rows], axis=axis)


def reference(fields, aggregation, operators, disaggregation, near_tile, near_operator, far_slot, far_operator, send_tiles):
    agg_full = aggregation.astype(jnp.float32)
    dis_full = disaggregation.astype(jnp.float32)
    tile_fields = fields.reshape(NTILES, TILE, Q, 2 * ILL)

    def aggregate(block):
        return jnp.einsum('kq,bqc->bkc', agg_full, stacked(block, 1).astype(jnp.float32)).astype(jnp.bfloat16)

    outgoing = lax.map(aggregate, tile_fields)

    def translate(target):
        sector_now = target // TPS
        near_src = sector_now * TPS + near_tile[target]
        src_sector = far_slot[target] // CAP
        position = far_slot[target] % CAP
        far_src = src_sector * TPS + send_tiles[src_sector, sector_now, position]
        sources = jnp.concatenate([near_src, far_src]).astype(jnp.int32)
        chosen = jnp.concatenate([near_operator[target], far_operator[target]]).astype(jnp.int32)
        source_rows = stacked(outgoing[sources], 1).astype(jnp.float32)
        op_blocks = operators[chosen].astype(jnp.float32)
        return jnp.einsum('lkab,lbkc->akc', op_blocks, source_rows).astype(jnp.bfloat16)

    incoming = lax.map(translate, jnp.arange(NTILES, dtype=jnp.int32))

    def disaggregate(block):
        return jnp.einsum('qk,bkc->bqc', dis_full, stacked(block, 1).astype(jnp.float32)).astype(jnp.bfloat16)

    result = lax.map(disaggregate, incoming)
    return result.reshape(BOXES, Q, 2 * ILL)
```

```python
import functools

import jax
import jax.numpy as jnp
from jax import lax
from jax.experimental import pallas as pl
from jax.experimental.pallas import tpu as pltpu
from jax.sharding import PartitionSpec as P

MESH = pl.DeviceIdType.MESH
F32 = jnp.float32
BF16 = jnp.bfloat16


def turned(x):
    half = x.shape[1] // 2
    lane = lax.broadcasted_iota(jnp.int32, x.shape, 1)
    swapped = pltpu.roll(x, half, 1)
    return jnp.where(lane < half, -swapped, swapped)


def exchange(
    sizes,
    fields,
    aggregation,
    operators,
    near_tile,
    near_op,
    far_slot,
    far_op,
    send_tiles,
    ret,
    fields_v,
    ops_v,
    stage32,
    stage,
    *scratch,
):
    sectors, dirs = sizes
    boxes, unknowns, lanes = fields_v.shape
    here = operators.shape[1]
    own, own_low, sendbuf, far, far_low = (
        scratch[i * here : (i + 1) * here] for i in range(5)
    )
    acc, inc, load_sem, send_sem, recv_sem = scratch[5 * here :]
    tiles, rows, _ = own[0].shape
    slots = far[0].shape[0]
    cap = slots // sectors
    me_s, me_d = lax.axis_index("sector"), lax.axis_index("dir")

    barrier = pltpu.get_barrier_semaphore()

    def greet_sector(i, carry):
        peer = lax.rem(me_s + i, sectors)
        pl.semaphore_signal(barrier, inc=1, device_id=(peer, me_d), device_id_type=MESH)
        return carry

    def greet_dir(i, carry):
        peer = lax.rem(me_d + i, dirs)
        pl.semaphore_signal(barrier, inc=1, device_id=(me_s, peer), device_id_type=MESH)
        return carry

    lax.fori_loop(1, sectors, greet_sector, 0)
    lax.fori_loop(1, dirs, greet_dir, 0)

    load_fields = pltpu.make_async_copy(fields, fields_v, load_sem.at[0])
    load_ops = pltpu.make_async_copy(operators, ops_v, load_sem.at[1])
    load_fields.start()
    load_ops.start()

    half = aggregation.shape[0]
    agg = jnp.concatenate([aggregation[:, :unknowns], aggregation[:, unknowns:]], axis=0)
    load_fields.wait()

    def aggregate(b, carry):
        both = jnp.dot(agg, fields_v[b], preferred_element_type=F32)
        stage32[pl.ds(b, half, stride=boxes), :] = both[:half] + turned(both[half:])
        return carry

    lax.fori_loop(0, boxes, aggregate, 0, unroll=4)

    def narrow(k, carry):
        stage[k] = stage32[pl.ds(k * boxes, boxes), :].astype(BF16)
        return carry

    lax.fori_loop(0, half, narrow, 0, unroll=4)

    pl.semaphore_wait(barrier, sectors + dirs - 2)

    tile_of, row_of = me_d * boxes // rows, lax.rem(me_d * boxes, rows)

    def scatter_out(k):
        def body(i, carry):
            peer = lax.rem(me_d + i, dirs)
            pltpu.make_async_remote_copy(
                src_ref=stage.at[peer * here + k],
                dst_ref=own[k].at[tile_of, pl.ds(row_of, boxes)],
                send_sem=send_sem.at[0],
                recv_sem=recv_sem.at[0, k],
                device_id=(me_s, peer),
                device_id_type=MESH,
            ).start()
            return carry

        lax.fori_loop(1, dirs, body, 0)
        own[k][tile_of, pl.ds(row_of, boxes), :] = stage[me_d * here + k]

    def wait_rows(ref, sem):
        pltpu.make_async_copy(ref, ref, sem).wait()

    def scatter_sector(k):
        wait_rows(stage.at[pl.ds(0, dirs - 1)], recv_sem.at[0, k])

        def pack(a, carry):
            for j in range(cap):
                sendbuf[k][a * cap + j] = own[k][send_tiles[me_s, j, a]]
            return carry

        lax.fori_loop(0, sectors, pack, 0)

        def body(i, carry):
            peer = lax.rem(me_s + i, sectors)
            pltpu.make_async_remote_copy(
                src_ref=sendbuf[k].at[pl.ds(peer * cap, cap)],
                dst_ref=far[k].at[pl.ds(me_s * cap, cap)],
                send_sem=send_sem.at[1],
                recv_sem=recv_sem.at[1, k],
                device_id=(peer, me_d),
                device_id_type=MESH,
            ).start()
            return carry

        for i in range(sectors // 2):
            body(sectors // 2 - i, 0)
            if i:
                body(sectors // 2 + i, 0)

    def turn(src, dst, count):
        def body(t, carry):
            dst[t] = turned(src[t].astype(F32)).astype(BF16)
            return carry

        lax.fori_loop(0, count, body, 0, unroll=2)

    def products(k, t, tile_ref, op_ref, high, low):
        total = None
        count = tile_ref.shape[1]
        for e in range(0, count, 2):
            left, right = [], []
            for f in (e, e + 1):
                left.append(ops_v[op_ref[t, f], k])
                src = tile_ref[t, f]
                right += [high[src], low[src]]
            part = jnp.dot(
                jnp.concatenate(left, axis=1),
                jnp.concatenate(right, axis=0),
                preferred_element_type=F32,
            )
            total = part if total is None else total + part
        return total

    def near(k):
        def body(t, carry):
            acc[k, t] = products(k, t, near_tile, near_op, own[k], own_low[k])
            return carry

        lax.fori_loop(0, tiles, body, 0)

    def far_and_return(k):
        wait_rows(far[k].at[pl.ds(0, slots - cap)], recv_sem.at[1, k])
        turn(far[k], far_low[k], slots)

        def body(t, carry):
            total = acc[k, t] + products(k, t, far_slot, far_op, far[k], far_low[k])
            inc[k, t] = total.astype(BF16)
            return carry

        lax.fori_loop(0, tiles, body, 0)

        def give(i, carry):
            peer = lax.rem(me_d + i, dirs)
            pltpu.make_async_remote_copy(
                src_ref=inc.at[k, peer * boxes // rows, pl.ds(lax.rem(peer * boxes, rows), boxes)],
                dst_ref=ret.at[me_d * here + k],
                send_sem=send_sem.at[2],
                recv_sem=recv_sem.at[2, k],
                device_id=(me_s, peer),
                device_id_type=MESH,
            ).start()
            return carry

        lax.fori_loop(1, dirs, give, 0)
        ret[me_d * here + k] = inc[k, tile_of, pl.ds(row_of, boxes), :]

    zero = jnp.zeros((cap, rows, lanes), BF16)
    for k in range(here):
        far[k][pl.ds(me_s * cap, cap)] = zero
    for k in range(here):
        scatter_out(k)
    for k in range(here):
        scatter_sector(k)
    for k in range(here):
        turn(own[k], own_low[k], tiles)
    load_ops.wait()
    for k in range(here):
        near(k)
    for k in range(here):
        far_and_return(k)
    for k in range(here):
        wait_rows(stage.at[pl.ds(0, dirs - 1)], recv_sem.at[2, k])
    for k in range(here):
        wait_rows(stage.at[pl.ds(0, dirs - 1)], send_sem.at[0])
        wait_rows(far[k].at[pl.ds(0, slots - cap)], send_sem.at[1])
        wait_rows(stage.at[pl.ds(0, dirs - 1)], send_sem.at[2])


def disaggregate(ret, disaggregation, out, wide):
    dirs, boxes, lanes = ret.shape
    count = out.shape[0]
    first = pl.program_id(0) * count

    @pl.when(pl.program_id(0) == 0)
    def _():
        def widen(k, carry):
            wide[pl.ds(k * boxes, boxes), :] = ret[k].astype(F32)
            return carry

        lax.fori_loop(0, dirs, widen, 0, unroll=4)

    matrix = disaggregation[...]
    for b in range(count):
        x = wide[pl.ds(first + b, dirs, stride=boxes), :]
        both = jnp.concatenate([x.astype(BF16), turned(x).astype(BF16)], axis=0)
        out[b] = jnp.dot(matrix, both, preferred_element_type=F32).astype(BF16)


def local(
    sizes,
    fields,
    aggregation,
    operators,
    disaggregation,
    near_tile,
    near_operator,
    far_slot,
    far_operator,
    send_tiles,
):
    boxes, unknowns, lanes = fields.shape
    here, rows = operators.shape[1], operators.shape[2]
    tiles = near_tile.shape[0]
    cap = send_tiles.shape[2]
    sectors, dirs = sizes
    all_dirs = here * dirs
    slots = sectors * cap
    anywhere = pl.BlockSpec(memory_space=pl.ANY)
    vmem = pl.BlockSpec(memory_space=pltpu.VMEM)
    smem = pl.BlockSpec(memory_space=pltpu.SMEM)
    ret = pl.pallas_call(
        functools.partial(exchange, sizes),
        out_shape=jax.ShapeDtypeStruct((all_dirs, boxes, lanes), BF16),
        in_specs=[anywhere, vmem, anywhere] + [smem] * 5,
        out_specs=vmem,
        scratch_shapes=[
            pltpu.VMEM((boxes, unknowns, lanes), BF16),
            pltpu.VMEM(operators.shape, BF16),
            pltpu.VMEM((all_dirs * boxes, lanes), F32),
            pltpu.VMEM((all_dirs, boxes, lanes), BF16),
            *[pltpu.VMEM((tiles, rows, lanes), BF16)] * (2 * here),
            *[pltpu.VMEM((slots, rows, lanes), BF16)] * (3 * here),
            pltpu.VMEM((here, tiles, rows, lanes), F32),
            pltpu.VMEM((here, tiles, rows, lanes), BF16),
            pltpu.SemaphoreType.DMA((2,)),
            pltpu.SemaphoreType.DMA((3,)),
            pltpu.SemaphoreType.DMA((3, here)),
        ],
        compiler_params=pltpu.CompilerParams(
            collective_id=0, has_side_effects=True, vmem_limit_bytes=40 << 20
        ),
    )(
        fields,
        aggregation,
        operators,
        near_tile,
        near_operator,
        far_slot,
        far_operator,
        jnp.swapaxes(send_tiles, 1, 2),
    )
    block = 8
    return pl.pallas_call(
        disaggregate,
        grid=(boxes // block,),
        out_shape=jax.ShapeDtypeStruct(fields.shape, BF16),
        in_specs=[vmem, vmem],
        out_specs=pl.BlockSpec((block, unknowns, lanes), lambda i: (i, 0, 0)),
        scratch_shapes=[pltpu.VMEM((all_dirs * boxes, lanes), F32)],
    )(ret, disaggregation)


def solution(mesh):
    placed = (
        P(("sector", "dir"), None, None),
        P(),
        P(None, "dir", None, None),
        P(),
        P("sector", None),
        P("sector", None),
        P("sector", None),
        P("sector", None),
        P(),
    )
    return jax.shard_map(
        functools.partial(local, (mesh.shape["sector"], mesh.shape["dir"])),
        mesh=mesh,
        in_specs=placed,
        out_specs=P(("sector", "dir"), None, None),
        check_vma=False,
    )
```

```python
import functools

import jax
import jax.numpy as jnp
from jax import lax
from jax.experimental import pallas as pl
from jax.experimental.pallas import tpu as pltpu
from jax.sharding import PartitionSpec as P

MESH = pl.DeviceIdType.MESH
F32 = jnp.float32
BF16 = jnp.bfloat16


def turned(x):
    half = x.shape[1] // 2
    lane = lax.broadcasted_iota(jnp.int32, x.shape, 1)
    swapped = pltpu.roll(x, half, 1)
    return jnp.where(lane < half, -swapped, swapped)


def chunks_of(here, boxes):
    small = boxes // 2
    found = [(0, 0, small), (0, small, boxes - small)]
    return found + [(k, 0, boxes) for k in range(1, here)]


def exchange(sizes, fields_h, aggregation_h, operators_h, *refs):
    sectors, dirs = sizes
    tables_h, ret, refs = refs[:5], refs[5], refs[6:]
    aggregation, fields, ops, stage32, stage, acc, inc = refs[:7]
    tables = refs[7:12]
    near_tile, near_op, far_slot, far_op, send_tiles = tables
    load_sem, send_sem, recv_sem, back_sem, entered = refs[12:17]
    boxes, unknowns, lanes = fields.shape
    here, tiles, rows, _ = inc.shape
    own_full, far_full = refs[17 : 17 + here], refs[17 + here : 17 + 2 * here]
    chunks = chunks_of(here, boxes)
    count = len(chunks)
    rest = refs[17 + 2 * here :]
    own, sendbuf, far = (rest[i * count : (i + 1) * count] for i in range(3))
    slots = far_full[0].shape[0]
    cap = slots // sectors
    per = rows // boxes
    parts = load_sem.shape[0] - 7
    me_s, me_d = lax.axis_index("sector"), lax.axis_index("dir")
    my_tile, my_sub = me_d // per, lax.rem(me_d, per)

    barrier = pltpu.get_barrier_semaphore()

    reach = sectors // 4

    def greet_sector(i, carry):
        for shift in (i, sectors - i):
            peer = lax.rem(me_s + shift, sectors)
            pl.semaphore_signal(barrier, inc=1, device_id=(peer, me_d), device_id_type=MESH)
        return carry

    def greet_dir(i, carry):
        peer = lax.rem(me_d + i, dirs)
        pl.semaphore_signal(barrier, inc=1, device_id=(me_s, peer), device_id_type=MESH)
        return carry

    lax.fori_loop(1, reach + 1, greet_sector, 0)
    lax.fori_loop(1, dirs, greet_dir, 0)

    load_agg = pltpu.make_async_copy(aggregation_h, aggregation, load_sem.at[0])
    load_ops = pltpu.make_async_copy(operators_h, ops, load_sem.at[1])
    load_tables = [
        pltpu.make_async_copy(src, dst, load_sem.at[2 + i])
        for i, (src, dst) in enumerate(zip(tables_h, tables))
    ]
    share = boxes // parts
    load_fields = [
        pltpu.make_async_copy(
            fields_h.at[pl.ds(i * share, share)],
            fields.at[pl.ds(i * share, share)],
            load_sem.at[7 + i],
        )
        for i in range(parts)
    ]
    for load in [load_agg, *load_fields, *load_tables, load_ops]:
        load.start()
    load_agg.wait()
    half = aggregation.shape[0]
    agg = jnp.concatenate([aggregation[:, :unknowns], aggregation[:, unknowns:]], axis=0)

    def aggregate(b, carry):
        both = jnp.dot(agg, fields[b], preferred_element_type=F32)
        stage32[pl.ds(b, half, stride=boxes), :] = both[:half] + turned(both[half:])
        return carry

    for i in range(parts):
        load_fields[i].wait()
        lax.fori_loop(i * share, (i + 1) * share, aggregate, 0, unroll=4)

    def narrow(k, carry):
        stage[k] = stage32[pl.ds(k * boxes, boxes), :].astype(BF16)
        return carry

    lax.fori_loop(0, half, narrow, 0, unroll=4)
    for load in load_tables:
        load.wait()

    pl.semaphore_wait(barrier, 2 * reach + dirs - 1)
    for shift in (reach, sectors - reach):
        peer = lax.rem(me_s + shift, sectors)
        pl.semaphore_signal(entered, inc=1, device_id=(peer, me_d), device_id_type=MESH)

    def wait_rows(ref, sem):
        pltpu.make_async_copy(ref, ref, sem).wait()

    def wait_dirs(c, sem):
        wait_rows(stage.at[pl.ds(0, dirs - 1), pl.ds(0, chunks[c][2])], sem)

    def wait_sectors(c, sem):
        wait_rows(far[c].at[pl.ds(0, slots - cap)], sem)

    side = 4 if tiles == 16 else 1

    def tile_at(i):
        if side == 1:
            return lax.rem(my_tile + 1 + i, tiles)
        j, h = i // side, lax.rem(i, side)
        y = lax.rem(my_tile // side + 2 + j * (j + 1) // 2, side)
        x = lax.rem(lax.rem(my_tile, side) + 2 + h * (h + 1) // 2, side)
        return y * side + x

    def scatter_dir(c):
        k, low, size = chunks[c]

        def copy_to(peer):
            pltpu.make_async_remote_copy(
                src_ref=stage.at[peer * here + k, pl.ds(low, size)],
                dst_ref=own[c].at[my_tile, pl.ds(my_sub * size, size)],
                send_sem=send_sem.at[0, c],
                recv_sem=recv_sem.at[0, c],
                device_id=(me_s, peer),
                device_id_type=MESH,
            ).start()

        def body(i, carry):
            for s in range(per):
                copy_to(tile_at(i) * per + s)
            return carry

        lax.fori_loop(0, tiles - 1, body, 0)
        for s in range(1, per):
            copy_to(my_tile * per + lax.rem(my_sub + s, per))
        own[c][my_tile, pl.ds(my_sub * size, size), :] = stage[
            me_d * here + k, pl.ds(low, size), :
        ]

    def scatter_sector(c):
        wait_dirs(c, recv_sem.at[0, c])
        if c == 0:
            pl.semaphore_wait(entered, 2)

        def pack(a, carry):
            for j in range(cap):
                sendbuf[c][a * cap + j] = own[c][send_tiles[me_s, j, a]]
            return carry

        lax.fori_loop(0, sectors, pack, 0, unroll=2)

        def send(i):
            peer = lax.rem(me_s + i, sectors)
            pltpu.make_async_remote_copy(
                src_ref=sendbuf[c].at[pl.ds(peer * cap, cap)],
                dst_ref=far[c].at[pl.ds(me_s * cap, cap)],
                send_sem=send_sem.at[1, c],
                recv_sem=recv_sem.at[1, c],
                device_id=(peer, me_d),
                device_id_type=MESH,
            ).start()

        for turn in range(4):
            for i in range(sectors // 2):
                for shift in (sectors // 2 - i, sectors // 2 + i)[: 1 + (i > 0)]:
                    peer = lax.rem(me_s + shift, sectors)
                    rank = jnp.minimum(peer // 2, 3)
                    pl.when(rank == turn)(functools.partial(send, shift))

    def place(src, dst, c, total):
        _, low, size = chunks[c]

        def body(t, carry):
            piece = src[t]
            other = turned(piece.astype(F32)).astype(BF16)
            for s in range(per):
                start = s * boxes + low
                dst[t, start : start + size, :] = piece[s * size : (s + 1) * size]
                dst[t, rows + start : rows + start + size, :] = other[s * size : (s + 1) * size]
            return carry

        lax.fori_loop(0, total, body, 0, unroll=2)

    def products(k, t, tile_ref, op_ref, full):
        total = None
        for e in range(0, tile_ref.shape[1], 2):
            left = [ops[op_ref[t, f], k] for f in (e, e + 1)]
            right = [full[tile_ref[t, f]] for f in (e, e + 1)]
            part = jnp.dot(
                jnp.concatenate(left, axis=1),
                jnp.concatenate(right, axis=0),
                preferred_element_type=F32,
            )
            total = part if total is None else total + part
        return total

    def near(k):
        def body(t, carry):
            acc[k, t] = products(k, t, near_tile, near_op, own_full[k])
            return carry

        lax.fori_loop(0, tiles, body, 0)

    def give(k, tile, sub):
        pltpu.make_async_remote_copy(
            src_ref=inc.at[k, tile, pl.ds(sub * boxes, boxes)],
            dst_ref=ret.at[me_d * here + k],
            send_sem=back_sem.at[0, k],
            recv_sem=back_sem.at[1, k],
            device_id=(me_s, tile * per + sub),
            device_id_type=MESH,
        ).start()

    def far_and_return(k):
        def body(i, carry):
            t = tile_at(i)
            total = acc[k, t] + products(k, t, far_slot, far_op, far_full[k])
            inc[k, t] = total.astype(BF16)

            @pl.when(i > 0)
            def _():
                for s in range(per):
                    give(k, tile_at(i - 1), s)

            return carry

        lax.fori_loop(0, tiles, body, 0)
        for s in range(1, per):
            give(k, my_tile, lax.rem(my_sub + s, per))
        ret[me_d * here + k] = inc[k, my_tile, pl.ds(my_sub * boxes, boxes), :]

    scatter_dir(0)
    for c in range(count):
        scatter_sector(c)
        if c + 1 < count:
            scatter_dir(c + 1)
    for c in range(count):
        place(own[c], own_full[chunks[c][0]], c, tiles)
    load_ops.wait()
    for k in range(here):
        near(k)
    for k in range(here):
        for c in range(count):
            if chunks[c][0] == k:
                wait_sectors(c, recv_sem.at[1, c])
                place(far[c], far_full[k], c, slots)
        far_and_return(k)
    for c in range(count):
        wait_dirs(c, send_sem.at[0, c])
        wait_sectors(c, send_sem.at[1, c])
    for k in range(here):
        wait_rows(stage.at[pl.ds(0, dirs - 1)], back_sem.at[0, k])
        wait_rows(stage.at[pl.ds(0, dirs - 1)], back_sem.at[1, k])


def disaggregate(ret, disaggregation, out, wide):
    dirs, boxes, lanes = ret.shape
    count = out.shape[0]
    first = pl.program_id(0) * count

    @pl.when(pl.program_id(0) == 0)
    def _():
        def widen(k, carry):
            wide[pl.ds(k * boxes, boxes), :] = ret[k].astype(F32)
            return carry

        lax.fori_loop(0, dirs, widen, 0, unroll=4)

    matrix = disaggregation[...]
    for b in range(count):
        x = wide[pl.ds(first + b, dirs, stride=boxes), :]
        both = jnp.concatenate([x.astype(BF16), turned(x).astype(BF16)], axis=0)
        out[b] = jnp.dot(matrix, both, preferred_element_type=F32).astype(BF16)


def local(
    sizes,
    fields,
    aggregation,
    operators,
    disaggregation,
    near_tile,
    near_operator,
    far_slot,
    far_operator,
    send_tiles,
):
    boxes, unknowns, lanes = fields.shape
    here, rows = operators.shape[1], operators.shape[2]
    tiles = near_tile.shape[0]
    cap = send_tiles.shape[2]
    sectors, dirs = sizes
    all_dirs = here * dirs
    slots = sectors * cap
    per = rows // boxes
    chunks = chunks_of(here, boxes)
    hbm = pl.BlockSpec(memory_space=pltpu.HBM)
    vmem = pl.BlockSpec(memory_space=pltpu.VMEM)
    tables = (near_tile, near_operator, far_slot, far_operator, jnp.swapaxes(send_tiles, 1, 2))
    ret = pl.pallas_call(
        functools.partial(exchange, sizes),
        out_shape=jax.ShapeDtypeStruct((all_dirs, boxes, lanes), BF16),
        in_specs=[hbm] * 8,
        out_specs=vmem,
        scratch_shapes=[
            pltpu.VMEM(aggregation.shape, BF16),
            pltpu.VMEM((boxes, unknowns, lanes), BF16),
            pltpu.VMEM(operators.shape, BF16),
            pltpu.VMEM((all_dirs * boxes, lanes), F32),
            pltpu.VMEM((all_dirs, boxes, lanes), BF16),
            pltpu.VMEM((here, tiles, rows, lanes), F32),
            pltpu.VMEM((here, tiles, rows, lanes), BF16),
            *[pltpu.SMEM(table.shape, jnp.int32) for table in tables],
            pltpu.SemaphoreType.DMA((7 + 4,)),
            pltpu.SemaphoreType.DMA((2, len(chunks))),
            pltpu.SemaphoreType.DMA((2, len(chunks))),
            pltpu.SemaphoreType.DMA((2, here)),
            pltpu.SemaphoreType.REGULAR,
            *[pltpu.VMEM((tiles, 2 * rows, lanes), BF16)] * here,
            *[pltpu.VMEM((slots, 2 * rows, lanes), BF16)] * here,
            *[pltpu.VMEM((tiles, per * size, lanes), BF16) for _, _, size in chunks],
            *[pltpu.VMEM((slots, per * size, lanes), BF16) for _, _, size in chunks] * 2,
        ],
        compiler_params=pltpu.CompilerParams(
            collective_id=0, has_side_effects=True
        ),
    )(fields, aggregation, operators, *tables)
    block = 8
    return pl.pallas_call(
        disaggregate,
        grid=(boxes // block,),
        out_shape=jax.ShapeDtypeStruct(fields.shape, BF16),
        in_specs=[vmem, vmem],
        out_specs=pl.BlockSpec((block, unknowns, lanes), lambda i: (i, 0, 0)),
        scratch_shapes=[pltpu.VMEM((all_dirs * boxes, lanes), F32)],
        compiler_params=pltpu.CompilerParams(vmem_limit_bytes=16 << 20),
    )(ret, disaggregation)


def solution(mesh):
    placed = (
        P(("sector", "dir"), None, None),
        P(),
        P(None, "dir", None, None),
        P(),
        P("sector", None),
        P("sector", None),
        P("sector", None),
        P("sector", None),
        P(),
    )
    return jax.shard_map(
        functools.partial(local, (mesh.shape["sector"], mesh.shape["dir"])),
        mesh=mesh,
        in_specs=placed,
        out_specs=P(("sector", "dir"), None, None),
        check_vma=False,
    )
```

```python
import functools

import jax
import jax.numpy as jnp
from jax import lax
from jax.experimental import pallas as pl
from jax.experimental.pallas import tpu as pltpu
from jax.sharding import PartitionSpec as P

MESH = pl.DeviceIdType.MESH
F32 = jnp.float32
BF16 = jnp.bfloat16


def turned(x):
    half = x.shape[1] // 2
    lane = lax.broadcasted_iota(jnp.int32, x.shape, 1)
    swapped = pltpu.roll(x, half, 1)
    return jnp.where(lane < half, -swapped, swapped)


def chunks_of(here, boxes):
    small = boxes // 2
    found = [(0, 0, small), (0, small, boxes - small)]
    return found + [(k, 0, boxes) for k in range(1, here)]


def exchange(sizes, fields_h, aggregation_h, operators_h, *refs):
    sectors, dirs = sizes
    tables_h, ret, refs = refs[:5], refs[5], refs[6:]
    aggregation, fields, ops, stage32, stage, acc, inc = refs[:7]
    tables = refs[7:12]
    near_tile, near_op, far_slot, far_op, send_tiles = tables
    load_sem, send_sem, recv_sem, back_sem, entered = refs[12:17]
    refs = refs[17:]
    boxes, unknowns, lanes = fields.shape
    here, tiles, rows, _ = inc.shape
    own_full, far_full = (refs[i * here : (i + 1) * here] for i in range(2))
    chunks = chunks_of(here, boxes)
    count = len(chunks)
    rest = refs[2 * here :]
    own, sendbuf, far = (rest[i * count : (i + 1) * count] for i in range(3))
    slots = far_full[0].shape[0]
    cap = slots // sectors
    per = rows // boxes
    parts = load_sem.shape[0] - 7 - here
    me_s, me_d = lax.axis_index("sector"), lax.axis_index("dir")
    my_tile, my_sub = lax.div(me_d, per), lax.rem(me_d, per)

    load_agg = pltpu.make_async_copy(aggregation_h, aggregation, load_sem.at[0])
    load_ops = pltpu.make_async_copy(operators_h, ops, load_sem.at[1])
    load_tables = [
        pltpu.make_async_copy(src, dst, load_sem.at[2 + i])
        for i, (src, dst) in enumerate(zip(tables_h, tables))
    ]
    share = boxes // parts
    load_fields = [
        pltpu.make_async_copy(
            fields_h.at[pl.ds(i * share, share)],
            fields.at[pl.ds(i * share, share)],
            load_sem.at[7 + here + i],
        )
        for i in range(parts)
    ]
    for load in [load_agg, *load_fields, *load_tables, load_ops]:
        load.start()
    barrier = pltpu.get_barrier_semaphore()

    reach = sectors // 4

    def greet_sector(i, carry):
        for shift in (i, sectors - i):
            peer = lax.rem(me_s + shift, sectors)
            pl.semaphore_signal(barrier, inc=1, device_id=(peer, me_d), device_id_type=MESH)
        return carry

    def greet_dir(i, carry):
        peer = lax.rem(me_d + i, dirs)
        pl.semaphore_signal(barrier, inc=1, device_id=(me_s, peer), device_id_type=MESH)
        return carry

    lax.fori_loop(1, reach + 1, greet_sector, 0)
    lax.fori_loop(1, dirs, greet_dir, 0)

    load_agg.wait()
    half = aggregation.shape[0]
    agg = jnp.concatenate([aggregation[:, :unknowns], aggregation[:, unknowns:]], axis=0)

    def aggregate(b, carry):
        both = jnp.dot(agg, fields[b], preferred_element_type=F32)
        stage32[pl.ds(b, half, stride=boxes), :] = both[:half] + turned(both[half:])
        return carry

    def aggregate_part(i):
        load_fields[i].wait()
        lax.fori_loop(i * share, (i + 1) * share, aggregate, 0, unroll=4)

    def narrow(c):
        k, low, size = chunks[c]

        def body(d, carry):
            row = pl.multiple_of((d * here + k) * boxes + low, 8)
            stage[d * here + k, low : low + size, :] = stage32[pl.ds(row, size), :].astype(BF16)
            return carry

        lax.fori_loop(0, dirs, body, 0, unroll=4)

    cut = parts // 2
    for i in range(cut):
        aggregate_part(i)
    narrow(0)
    pl.semaphore_wait(barrier, 2 * reach + dirs - 1)

    for shift in (reach, sectors - reach):
        peer = lax.rem(me_s + shift, sectors)
        pl.semaphore_signal(entered, inc=1, device_id=(peer, me_d), device_id_type=MESH)

    def wait_rows(ref, sem):
        pltpu.make_async_copy(ref, ref, sem).wait()

    def wait_dirs(c, sem):
        wait_rows(stage.at[pl.ds(0, dirs - 1), pl.ds(0, chunks[c][2])], sem)

    def wait_sectors(c, sem):
        wait_rows(far[c].at[pl.ds(0, slots - cap)], sem)

    side = 4 if tiles == 16 else 1

    def tile_at(i):
        if side == 1:
            return lax.rem(my_tile + 1 + i, tiles)
        j, h = lax.div(i, side), lax.rem(i, side)
        y = lax.rem(lax.div(my_tile, side) + 2 + lax.div(j * (j + 1), 2), side)
        x = lax.rem(lax.rem(my_tile, side) + 2 + lax.div(h * (h + 1), 2), side)
        return y * side + x

    def scatter_dir(c):
        k, low, size = chunks[c]

        def copy_to(peer):
            pltpu.make_async_remote_copy(
                src_ref=stage.at[peer * here + k, pl.ds(low, size)],
                dst_ref=own[c].at[my_tile, pl.ds(my_sub * size, size)],
                send_sem=send_sem.at[0, c],
                recv_sem=recv_sem.at[0, c],
                device_id=(me_s, peer),
                device_id_type=MESH,
            ).start()

        def body(i, carry):
            for s in range(per):
                copy_to(tile_at(i) * per + s)
            return carry

        lax.fori_loop(0, tiles - 1, body, 0)
        for s in range(1, per):
            copy_to(my_tile * per + lax.rem(my_sub + s, per))
        own[c][my_tile, pl.ds(my_sub * size, size), :] = stage[
            me_d * here + k, pl.ds(low, size), :
        ]

    def scatter_sector(c):
        wait_dirs(c, recv_sem.at[0, c])
        if c == 0:
            pl.semaphore_wait(entered, 2)

        def pack(a, carry):
            for j in range(cap):
                sendbuf[c][a * cap + j] = own[c][send_tiles[me_s, j, a]]
            return carry

        lax.fori_loop(0, sectors, pack, 0, unroll=2)

        def send(i):
            peer = lax.rem(me_s + i, sectors)
            pltpu.make_async_remote_copy(
                src_ref=sendbuf[c].at[pl.ds(peer * cap, cap)],
                dst_ref=far[c].at[pl.ds(me_s * cap, cap)],
                send_sem=send_sem.at[1, c],
                recv_sem=recv_sem.at[1, c],
                device_id=(peer, me_d),
                device_id_type=MESH,
            ).start()

        def send_low(p, carry):
            pl.when(p != me_s)(lambda: send(lax.rem(p + sectors - me_s, sectors)))
            return carry

        low_half = sectors
        lax.fori_loop(0, low_half, send_low, 0)

    def place(src, dst, c, total):
        _, low, size = chunks[c]

        def body(t, carry):
            piece = src[t]
            other = turned(piece.astype(F32)).astype(BF16)
            for s in range(per):
                start = s * boxes + low
                dst[t, start : start + size, :] = piece[s * size : (s + 1) * size]
                dst[t, rows + start : rows + start + size, :] = other[s * size : (s + 1) * size]
            return carry

        lax.fori_loop(0, total, body, 0, unroll=2)

    def products(k, t, tile_ref, op_ref, full):
        total = None
        for e in range(0, tile_ref.shape[1], 2):
            left = [ops[op_ref[t, f], k] for f in (e, e + 1)]
            right = [full[tile_ref[t, f]] for f in (e, e + 1)]
            part = jnp.dot(
                jnp.concatenate(left, axis=1),
                jnp.concatenate(right, axis=0),
                preferred_element_type=F32,
            )
            total = part if total is None else total + part
        return total

    def near(k):
        def body(t, carry):
            acc[k, t] = products(k, t, near_tile, near_op, own_full[k])
            return carry

        lax.fori_loop(0, tiles, body, 0)

    def give(k, tile, sub):
        pltpu.make_async_remote_copy(
            src_ref=inc.at[k, tile, pl.ds(sub * boxes, boxes)],
            dst_ref=ret.at[me_d * here + k],
            send_sem=back_sem.at[0, k],
            recv_sem=back_sem.at[1, k],
            device_id=(me_s, tile * per + sub),
            device_id_type=MESH,
        ).start()

    def far_and_return(k):
        def body(i, carry):
            t = tile_at(i)
            total = acc[k, t] + products(k, t, far_slot, far_op, far_full[k])
            inc[k, t] = total.astype(BF16)

            @pl.when(i > 0)
            def _():
                for s in range(per):
                    give(k, tile_at(i - 1), s)

            return carry

        lax.fori_loop(0, tiles, body, 0)
        for s in range(1, per):
            give(k, my_tile, lax.rem(my_sub + s, per))
        keep = pltpu.make_async_copy(
            inc.at[k, my_tile, pl.ds(my_sub * boxes, boxes)],
            ret.at[me_d * here + k],
            load_sem.at[7 + k],
        )
        keep.start()
        return keep

    scatter_dir(0)
    for i in range(cut, parts):
        aggregate_part(i)
    for c in range(1, count):
        narrow(c)
    for load in load_tables:
        load.wait()
    for c in range(count):
        scatter_sector(c)
        if c + 1 < count:
            scatter_dir(c + 1)
    for c in range(count):
        place(own[c], own_full[chunks[c][0]], c, tiles)
    load_ops.wait()
    for k in range(here):
        near(k)
    keeps = []
    for k in range(here):
        for c in range(count):
            if chunks[c][0] == k:
                wait_sectors(c, recv_sem.at[1, c])
                place(far[c], far_full[k], c, slots)
        keeps.append(far_and_return(k))
    for c in range(count):
        wait_dirs(c, send_sem.at[0, c])
        wait_sectors(c, send_sem.at[1, c])
    for k in range(here):
        wait_rows(stage.at[pl.ds(0, dirs - 1)], back_sem.at[0, k])
        wait_rows(stage.at[pl.ds(0, dirs - 1)], back_sem.at[1, k])
    for keep in keeps:
        keep.wait()


def disaggregate(ret_h, matrix_h, out_h, ret, matrix_v, wide, out, load_sem, store_sem):
    dirs, boxes, lanes = ret.shape
    parts = store_sem.shape[0]
    part, share = dirs // parts, boxes // parts
    loads = [
        pltpu.make_async_copy(
            ret_h.at[pl.ds(i * part, part)], ret.at[pl.ds(i * part, part)], load_sem.at[i]
        )
        for i in range(parts)
    ]
    load_matrix = pltpu.make_async_copy(matrix_h, matrix_v, load_sem.at[parts])
    for load in [*loads, load_matrix]:
        load.start()

    def widen(k, carry):
        wide[pl.ds(pl.multiple_of(k * boxes, 8), boxes), :] = ret[k].astype(F32)
        return carry

    for i in range(parts):
        loads[i].wait()
        lax.fori_loop(i * part, (i + 1) * part, widen, 0, unroll=4)
    load_matrix.wait()
    matrix = matrix_v[...]

    def body(b):
        x = wide[pl.ds(b, dirs, stride=boxes), :]
        both = jnp.concatenate([x.astype(BF16), turned(x).astype(BF16)], axis=0)
        out[b] = jnp.dot(matrix, both, preferred_element_type=F32).astype(BF16)

    stores = []
    for i in range(parts):
        for b in range(i * share, (i + 1) * share):
            body(b)
        store = pltpu.make_async_copy(
            out.at[pl.ds(i * share, share)], out_h.at[pl.ds(i * share, share)], store_sem.at[i]
        )
        store.start()
        stores.append(store)
    for store in stores:
        store.wait()


def local(
    sizes,
    fields,
    aggregation,
    operators,
    disaggregation,
    near_tile,
    near_operator,
    far_slot,
    far_operator,
    send_tiles,
):
    boxes, unknowns, lanes = fields.shape
    here, rows = operators.shape[1], operators.shape[2]
    tiles = near_tile.shape[0]
    cap = send_tiles.shape[2]
    sectors, dirs = sizes
    all_dirs = here * dirs
    slots = sectors * cap
    per = rows // boxes
    chunks = chunks_of(here, boxes)
    hbm = pl.BlockSpec(memory_space=pltpu.HBM)
    tables = (near_tile, near_operator, far_slot, far_operator, jnp.swapaxes(send_tiles, 1, 2))
    ret = pl.pallas_call(
        functools.partial(exchange, sizes),
        out_shape=jax.ShapeDtypeStruct((all_dirs, boxes, lanes), BF16),
        in_specs=[hbm] * 8,
        out_specs=hbm,
        scratch_shapes=[
            pltpu.VMEM(aggregation.shape, BF16),
            pltpu.VMEM((boxes, unknowns, lanes), BF16),
            pltpu.VMEM(operators.shape, BF16),
            pltpu.VMEM((all_dirs * boxes, lanes), F32),
            pltpu.VMEM((all_dirs, boxes, lanes), BF16),
            pltpu.VMEM((here, tiles, rows, lanes), F32),
            pltpu.VMEM((here, tiles, rows, lanes), BF16),
            *[pltpu.SMEM(table.shape, jnp.int32) for table in tables],
            pltpu.SemaphoreType.DMA((7 + here + 4,)),
            pltpu.SemaphoreType.DMA((2, len(chunks))),
            pltpu.SemaphoreType.DMA((2, len(chunks))),
            pltpu.SemaphoreType.DMA((2, here)),
            pltpu.SemaphoreType.REGULAR,
            *[pltpu.VMEM((tiles, 2 * rows, lanes), BF16)] * here,
            *[pltpu.VMEM((slots, 2 * rows, lanes), BF16)] * here,
            *[pltpu.VMEM((tiles, per * size, lanes), BF16) for _, _, size in chunks],
            *[pltpu.VMEM((slots, per * size, lanes), BF16) for _, _, size in chunks] * 2,
        ],
        compiler_params=pltpu.CompilerParams(
            collective_id=0, has_side_effects=True
        ),
    )(fields, aggregation, operators, *tables)
    return pl.pallas_call(
        disaggregate,
        out_shape=jax.ShapeDtypeStruct(fields.shape, BF16),
        in_specs=[hbm, hbm],
        out_specs=hbm,
        scratch_shapes=[
            pltpu.VMEM((all_dirs, boxes, lanes), BF16),
            pltpu.VMEM(disaggregation.shape, BF16),
            pltpu.VMEM((all_dirs * boxes, lanes), F32),
            pltpu.VMEM(fields.shape, BF16),
            pltpu.SemaphoreType.DMA((5,)),
            pltpu.SemaphoreType.DMA((4,)),
        ],
    )(ret, disaggregation)


def solution(mesh):
    placed = (
        P(("sector", "dir"), None, None),
        P(),
        P(None, "dir", None, None),
        P(),
        P("sector", None),
        P("sector", None),
        P("sector", None),
        P("sector", None),
        P(),
    )
    return jax.shard_map(
        functools.partial(local, (mesh.shape["sector"], mesh.shape["dir"])),
        mesh=mesh,
        in_specs=placed,
        out_specs=P(("sector", "dir"), None, None),
        check_vma=False,
    )
```

```python
import functools

import jax
import jax.numpy as jnp
from jax import lax
from jax.experimental import pallas as pl
from jax.experimental.pallas import tpu as pltpu
from jax.sharding import PartitionSpec as P

MESH = pl.DeviceIdType.MESH
F32 = jnp.float32
BF16 = jnp.bfloat16


def turned(x):
    half = x.shape[1] // 2
    lane = lax.broadcasted_iota(jnp.int32, x.shape, 1)
    swapped = pltpu.roll(x, half, 1)
    return jnp.where(lane < half, -swapped, swapped)


def chunks_of(here, boxes):
    small = boxes // 2
    found = [(0, 0, small), (0, small, boxes - small)]
    return found + [(k, 0, boxes) for k in range(1, here)]


def exchange(sizes, fields_h, aggregation_h, operators_h, *refs):
    sectors, dirs = sizes
    tables_h, ret, refs = refs[:5], refs[5], refs[6:]
    aggregation, fields, ops, stage32, stage, acc, inc = refs[:7]
    tables = refs[7:12]
    near_tile, near_op, far_slot, far_op, send_tiles = tables
    load_sem, send_sem, recv_sem, back_sem, entered = refs[12:17]
    refs = refs[17:]
    boxes, unknowns, lanes = fields.shape
    here, tiles, rows, _ = inc.shape
    own_full, far_full = (refs[i * here : (i + 1) * here] for i in range(2))
    chunks = chunks_of(here, boxes)
    count = len(chunks)
    rest = refs[2 * here :]
    own, sendbuf, far = (rest[i * count : (i + 1) * count] for i in range(3))
    slots = far_full[0].shape[0]
    cap = slots // sectors
    per = rows // boxes
    parts = load_sem.shape[0] - 7 - here
    me_s, me_d = lax.axis_index("sector"), lax.axis_index("dir")
    my_tile, my_sub = lax.div(me_d, per), lax.rem(me_d, per)

    load_agg = pltpu.make_async_copy(aggregation_h, aggregation, load_sem.at[0])
    load_ops = pltpu.make_async_copy(operators_h, ops, load_sem.at[1])
    load_tables = [
        pltpu.make_async_copy(src, dst, load_sem.at[2 + i])
        for i, (src, dst) in enumerate(zip(tables_h, tables))
    ]
    share = boxes // parts
    load_fields = [
        pltpu.make_async_copy(
            fields_h.at[pl.ds(i * share, share)],
            fields.at[pl.ds(i * share, share)],
            load_sem.at[7 + here + i],
        )
        for i in range(parts)
    ]
    for load in [load_agg, *load_fields, *load_tables, load_ops]:
        load.start()
    barrier = pltpu.get_barrier_semaphore()

    reach = sectors // 4

    def greet_sector(i, carry):
        for shift in (i, sectors - i):
            peer = lax.rem(me_s + shift, sectors)
            pl.semaphore_signal(barrier, inc=1, device_id=(peer, me_d), device_id_type=MESH)
        return carry

    def greet_dir(i, carry):
        peer = lax.rem(me_d + i, dirs)
        pl.semaphore_signal(barrier, inc=1, device_id=(me_s, peer), device_id_type=MESH)
        return carry

    lax.fori_loop(1, reach + 1, greet_sector, 0)
    lax.fori_loop(1, dirs, greet_dir, 0)

    load_agg.wait()
    half = aggregation.shape[0]
    agg = jnp.concatenate([aggregation[:, :unknowns], aggregation[:, unknowns:]], axis=0)

    def aggregate(b, carry):
        both = jnp.dot(agg, fields[b], preferred_element_type=F32)
        stage32[pl.ds(b, half, stride=boxes), :] = both[:half] + turned(both[half:])
        return carry

    def aggregate_part(i):
        load_fields[i].wait()
        lax.fori_loop(i * share, (i + 1) * share, aggregate, 0, unroll=4)

    def narrow(c):
        k, low, size = chunks[c]

        def body(d, carry):
            row = pl.multiple_of((d * here + k) * boxes + low, 8)
            stage[d * here + k, low : low + size, :] = stage32[pl.ds(row, size), :].astype(BF16)
            return carry

        lax.fori_loop(0, dirs, body, 0, unroll=4)

    cut = parts // 2
    for i in range(cut):
        aggregate_part(i)
    narrow(0)
    pl.semaphore_wait(barrier, 2 * reach + dirs - 1)

    for shift in (reach, sectors - reach):
        peer = lax.rem(me_s + shift, sectors)
        pl.semaphore_signal(entered, inc=1, device_id=(peer, me_d), device_id_type=MESH)

    def wait_rows(ref, sem):
        pltpu.make_async_copy(ref, ref, sem).wait()

    def wait_dirs(c, sem):
        wait_rows(stage.at[pl.ds(0, dirs - 1), pl.ds(0, chunks[c][2])], sem)

    def wait_sectors(c, sem):
        wait_rows(far[c].at[pl.ds(0, slots - cap)], sem)

    side = 4 if tiles == 16 else 1

    def tile_at(i):
        if side == 1:
            return lax.rem(my_tile + 1 + i, tiles)
        j, h = lax.div(i, side), lax.rem(i, side)
        y = lax.rem(lax.div(my_tile, side) + 2 + lax.div(j * (j + 1), 2), side)
        x = lax.rem(lax.rem(my_tile, side) + 2 + lax.div(h * (h + 1), 2), side)
        return y * side + x

    def return_at(i):
        return i

    def scatter_dir(c):
        k, low, size = chunks[c]

        def copy_to(peer):
            pltpu.make_async_remote_copy(
                src_ref=stage.at[peer * here + k, pl.ds(low, size)],
                dst_ref=own[c].at[my_tile, pl.ds(my_sub * size, size)],
                send_sem=send_sem.at[0, c],
                recv_sem=recv_sem.at[0, c],
                device_id=(me_s, peer),
                device_id_type=MESH,
            ).start()

        def body(i, carry):
            for s in range(per):
                copy_to(tile_at(i) * per + s)
            return carry

        lax.fori_loop(0, tiles - 1, body, 0)
        for s in range(1, per):
            copy_to(my_tile * per + lax.rem(my_sub + s, per))
        own[c][my_tile, pl.ds(my_sub * size, size), :] = stage[
            me_d * here + k, pl.ds(low, size), :
        ]

    def scatter_sector(c):
        wait_dirs(c, recv_sem.at[0, c])
        if c == 0:
            pl.semaphore_wait(entered, 2)

        def pack(a, carry):
            for j in range(cap):
                sendbuf[c][a * cap + j] = own[c][send_tiles[me_s, j, a]]
            return carry

        lax.fori_loop(0, sectors, pack, 0, unroll=2)

        def send(i):
            peer = lax.rem(me_s + i, sectors)
            pltpu.make_async_remote_copy(
                src_ref=sendbuf[c].at[pl.ds(peer * cap, cap)],
                dst_ref=far[c].at[pl.ds(me_s * cap, cap)],
                send_sem=send_sem.at[1, c],
                recv_sem=recv_sem.at[1, c],
                device_id=(peer, me_d),
                device_id_type=MESH,
            ).start()

        def send_low(p, carry):
            pl.when(p != me_s)(lambda: send(lax.rem(p + sectors - me_s, sectors)))
            return carry

        low_half = sectors
        lax.fori_loop(0, low_half, send_low, 0)

    def place(src, dst, c, total):
        _, low, size = chunks[c]

        def body(t, carry):
            piece = src[t]
            other = turned(piece.astype(F32)).astype(BF16)
            for s in range(per):
                start = s * boxes + low
                dst[t, start : start + size, :] = piece[s * size : (s + 1) * size]
                dst[t, rows + start : rows + start + size, :] = other[s * size : (s + 1) * size]
            return carry

        lax.fori_loop(0, total, body, 0, unroll=2)

    def products(k, t, tile_ref, op_ref, full):
        total = None
        for e in range(0, tile_ref.shape[1], 2):
            left = [ops[op_ref[t, f], k] for f in (e, e + 1)]
            right = [full[tile_ref[t, f]] for f in (e, e + 1)]
            part = jnp.dot(
                jnp.concatenate(left, axis=1),
                jnp.concatenate(right, axis=0),
                preferred_element_type=F32,
            )
            total = part if total is None else total + part
        return total

    def near(k):
        def body(t, carry):
            acc[k, t] = products(k, t, near_tile, near_op, own_full[k])
            return carry

        lax.fori_loop(0, tiles, body, 0)

    def give(k, tile, sub):
        pltpu.make_async_remote_copy(
            src_ref=inc.at[k, tile, pl.ds(sub * boxes, boxes)],
            dst_ref=ret.at[me_d * here + k],
            send_sem=back_sem.at[0, k],
            recv_sem=back_sem.at[1, k],
            device_id=(me_s, tile * per + sub),
            device_id_type=MESH,
        ).start()

    def far_and_return(k):
        def give_tile(t):
            for s in range(per):
                pl.when(t * per + s != me_d)(functools.partial(give, k, t, s))

        def body(i, carry):
            t = return_at(i)
            total = acc[k, t] + products(k, t, far_slot, far_op, far_full[k])
            inc[k, t] = total.astype(BF16)
            pl.when(i > 0)(lambda: give_tile(return_at(i - 1)))
            return carry

        lax.fori_loop(0, tiles, body, 0)
        give_tile(return_at(jnp.int32(tiles - 1)))
        keep = pltpu.make_async_copy(
            inc.at[k, my_tile, pl.ds(my_sub * boxes, boxes)],
            ret.at[me_d * here + k],
            load_sem.at[7 + k],
        )
        keep.start()
        return keep

    scatter_dir(0)
    for i in range(cut, parts):
        aggregate_part(i)
    for c in range(1, count):
        narrow(c)
    for load in load_tables:
        load.wait()
    for c in range(count):
        scatter_sector(c)
        if c + 1 < count:
            scatter_dir(c + 1)
    for c in range(count):
        place(own[c], own_full[chunks[c][0]], c, tiles)
    load_ops.wait()
    for k in range(here):
        near(k)
    keeps = []
    for k in range(here):
        for c in range(count):
            if chunks[c][0] == k:
                wait_sectors(c, recv_sem.at[1, c])
                place(far[c], far_full[k], c, slots)
        keeps.append(far_and_return(k))
    for c in range(count):
        wait_dirs(c, send_sem.at[0, c])
        wait_sectors(c, send_sem.at[1, c])
    for k in range(here):
        wait_rows(stage.at[pl.ds(0, dirs - 1)], back_sem.at[0, k])
        wait_rows(stage.at[pl.ds(0, dirs - 1)], back_sem.at[1, k])
    for keep in keeps:
        keep.wait()


def disaggregate(ret_h, matrix_h, out_h, ret, matrix_v, wide, out, load_sem, store_sem):
    dirs, boxes, lanes = ret.shape
    parts = store_sem.shape[0]
    part, share = dirs // parts, boxes // parts
    loads = [
        pltpu.make_async_copy(
            ret_h.at[pl.ds(i * part, part)], ret.at[pl.ds(i * part, part)], load_sem.at[i]
        )
        for i in range(parts)
    ]
    load_matrix = pltpu.make_async_copy(matrix_h, matrix_v, load_sem.at[parts])
    for load in [*loads, load_matrix]:
        load.start()

    def widen(k, carry):
        wide[pl.ds(pl.multiple_of(k * boxes, 8), boxes), :] = ret[k].astype(F32)
        return carry

    for i in range(parts):
        loads[i].wait()
        lax.fori_loop(i * part, (i + 1) * part, widen, 0, unroll=4)
    load_matrix.wait()
    matrix = matrix_v[...]

    def body(b):
        x = wide[pl.ds(b, dirs, stride=boxes), :]
        both = jnp.concatenate([x.astype(BF16), turned(x).astype(BF16)], axis=0)
        out[b] = jnp.dot(matrix, both, preferred_element_type=F32).astype(BF16)

    stores = []
    for i in range(parts):
        for b in range(i * share, (i + 1) * share):
            body(b)
        store = pltpu.make_async_copy(
            out.at[pl.ds(i * share, share)], out_h.at[pl.ds(i * share, share)], store_sem.at[i]
        )
        store.start()
        stores.append(store)
    for store in stores:
        store.wait()


def local(
    sizes,
    fields,
    aggregation,
    operators,
    disaggregation,
    near_tile,
    near_operator,
    far_slot,
    far_operator,
    send_tiles,
):
    boxes, unknowns, lanes = fields.shape
    here, rows = operators.shape[1], operators.shape[2]
    tiles = near_tile.shape[0]
    cap = send_tiles.shape[2]
    sectors, dirs = sizes
    all_dirs = here * dirs
    slots = sectors * cap
    per = rows // boxes
    chunks = chunks_of(here, boxes)
    hbm = pl.BlockSpec(memory_space=pltpu.HBM)
    tables = (near_tile, near_operator, far_slot, far_operator, jnp.swapaxes(send_tiles, 1, 2))
    ret = pl.pallas_call(
        functools.partial(exchange, sizes),
        out_shape=jax.ShapeDtypeStruct((all_dirs, boxes, lanes), BF16),
        in_specs=[hbm] * 8,
        out_specs=hbm,
        scratch_shapes=[
            pltpu.VMEM(aggregation.shape, BF16),
            pltpu.VMEM((boxes, unknowns, lanes), BF16),
            pltpu.VMEM(operators.shape, BF16),
            pltpu.VMEM((all_dirs * boxes, lanes), F32),
            pltpu.VMEM((all_dirs, boxes, lanes), BF16),
            pltpu.VMEM((here, tiles, rows, lanes), F32),
            pltpu.VMEM((here, tiles, rows, lanes), BF16),
            *[pltpu.SMEM(table.shape, jnp.int32) for table in tables],
            pltpu.SemaphoreType.DMA((7 + here + 4,)),
            pltpu.SemaphoreType.DMA((2, len(chunks))),
            pltpu.SemaphoreType.DMA((2, len(chunks))),
            pltpu.SemaphoreType.DMA((2, here)),
            pltpu.SemaphoreType.REGULAR,
            *[pltpu.VMEM((tiles, 2 * rows, lanes), BF16)] * here,
            *[pltpu.VMEM((slots, 2 * rows, lanes), BF16)] * here,
            *[pltpu.VMEM((tiles, per * size, lanes), BF16) for _, _, size in chunks],
            *[pltpu.VMEM((slots, per * size, lanes), BF16) for _, _, size in chunks] * 2,
        ],
        compiler_params=pltpu.CompilerParams(
            collective_id=0, has_side_effects=True
        ),
    )(fields, aggregation, operators, *tables)
    return pl.pallas_call(
        disaggregate,
        out_shape=jax.ShapeDtypeStruct(fields.shape, BF16),
        in_specs=[hbm, hbm],
        out_specs=hbm,
        scratch_shapes=[
            pltpu.VMEM((all_dirs, boxes, lanes), BF16),
            pltpu.VMEM(disaggregation.shape, BF16),
            pltpu.VMEM((all_dirs * boxes, lanes), F32),
            pltpu.VMEM(fields.shape, BF16),
            pltpu.SemaphoreType.DMA((5,)),
            pltpu.SemaphoreType.DMA((4,)),
        ],
    )(ret, disaggregation)


def solution(mesh):
    placed = (
        P(("sector", "dir"), None, None),
        P(),
        P(None, "dir", None, None),
        P(),
        P("sector", None),
        P("sector", None),
        P("sector", None),
        P("sector", None),
        P(),
    )
    return jax.shard_map(
        functools.partial(local, (mesh.shape["sector"], mesh.shape["dir"])),
        mesh=mesh,
        in_specs=placed,
        out_specs=P(("sector", "dir"), None, None),
        check_vma=False,
    )
```
